32 devices in a mesh: rep: 4 (over x, core), shard: 8 (over z, y).
Axes of the slice: x: 2, y: 2, z: 4, core: 2. Of those that a mesh axis runs over, the one named last changes fastest.
Arguments:
- tokens: bfloat16 [32, 448, 1024], P(('rep', 'shard')), may hold values from -6 to 6
- encoder_states: bfloat16 [32, 1500, 1024], P(('rep', 'shard')), may hold values from -6 to 6
- adapter_pick: int32 [32], P(('rep', 'shard')), may hold values from 0 to 7
- cotangent: bfloat16 [32, 448, 1024], P(('rep', 'shard')), may hold values from -6 to 6
- norm_gain: float32 [3, 1024], replicated, may hold values from 0.5 to 1.5
- norm_bias: float32 [3, 1024], replicated, may hold values from -3 to 3
- attention_weights: bfloat16 [6, 1024, 1024], P(None, 'shard'), may hold values from -0.1875 to 0.1875
- output_weights: bfloat16 [2, 1024, 1024], P(None, 'shard'), may hold values from -0.75 to 0.75
- expand_weight: bfloat16 [1024, 4096], P('shard'), may hold values from -0.1875 to 0.1875
- contract_weight: bfloat16 [4096, 1024], P('shard'), may hold values from -0.09375 to 0.09375
- adapter_down: bfloat16 [8, 8, 1024, 16], P(None, None, 'shard'), may hold values from -0.1875 to 0.1875
- adapter_up: bfloat16 [8, 8, 16, 1024], P(None, None, None, 'shard'), may hold values from -0.75 to 0.75
- expand_down: bfloat16 [8, 1024, 16], P(None, 'shard'), may hold values from -0.1875 to 0.1875
- expand_up: bfloat16 [8, 16, 4096], P(None, None, 'shard'), may hold values from -0.75 to 0.75
- contract_down: bfloat16 [8, 4096, 16], P(None, 'shard'), may hold values from -0.09375 to 0.09375
- contract_up: bfloat16 [8, 16, 1024], P(None, None, 'shard'), may hold values from -0.75 to 0.75
Outputs:
- layer_output: bfloat16 [32, 448, 1024], P(('rep', 'shard'))
- tokens_grad: float32 [32, 448, 1024], P(('rep', 'shard'))
- encoder_grad: float32 [32, 1500, 1024], P(('rep', 'shard'))
- adapter_down_grad: float32 [8, 8, 1024, 16], P(None, None, 'shard')
- adapter_up_grad: float32 [8, 8, 16, 1024], P(None, None, None, 'shard')
- expand_down_grad: float32 [8, 1024, 16], P(None, 'shard')
- expand_up_grad: float32 [8, 16, 4096], P(None, None, 'shard')
- contract_down_grad: float32 [8, 4096, 16], P(None, 'shard')
- contract_up_grad: float32 [8, 16, 1024], P(None, None, 'shard')
The draws below stay inside these ranges and needn't reach their ends.
All inputs are finite; a program needn't handle non-finite values.
Results may differ from the reference program's by a relative error of at most 0.02.
Values may be sent and summed in bfloat16 or wider, within the bound.
No kernel may reach another device: no remote copies, remote signals or barrier semaphores. Data moves between devices by JAX's collectives and lax.ppermute only.
A program may use at most 256 MiB of HBM per device.

```python
import jax
import jax.numpy as jnp
from jax import lax

D = 1024
HEADS = 16
HDIM = 64
FF = 4096
SEQ_LEN = 448
FRAMES = 1500
ADAPTERS = 8
RANK = 16
SEQS = 32


def with_ends(drawn, rng, smallest, high):
    spot = [jax.random.randint(jax.random.fold_in(rng, axis), (), 0, length) for axis, length in enumerate(drawn.shape)]
    widest = drawn.shape.index(max(drawn.shape))
    next_to = spot[:widest] + [(spot[widest] + 1) % drawn.shape[widest]] + spot[widest + 1:]
    return drawn.at[tuple(spot)].set(smallest).at[tuple(next_to)].set(high)


def block_scale(stream_key, shape, pieces, smallest, top_value):
    level, own = 1.0, jax.random.fold_in(stream_key, 6)
    for axis_at, parts in pieces:
        heights = jnp.exp(jax.random.uniform(jax.random.fold_in(own, axis_at), (parts,), jnp.float32, smallest / len(pieces), top_value / len(pieces)))
        level = level * jnp.repeat(heights, shape[axis_at] // parts).reshape([-1 if axis == axis_at else 1 for axis in range(len(shape))])
    return level


def noise(own_key, shape, spread, reach, pieces=(), kind=jnp.bfloat16):
    level = block_scale(own_key, shape, pieces, -0.22, 0.18) if pieces else 1.0
    array = jax.random.normal(own_key, shape, jnp.float32) * spread * level
    return jnp.minimum(jnp.maximum(array, -reach), reach).astype(kind)


def setup_inputs(seed: int = 0) -> dict:
    splits = jax.random.split(jax.random.key(seed), 17)
    tokens = noise(splits[0], (SEQS, SEQ_LEN, D), 1.0, 6.0, ((0, 32),))
    encoder_states = noise(splits[1], (SEQS, FRAMES, D), 1.0, 6.0, ((0, 32),))
    adapter_pick = with_ends(jax.random.randint(splits[2], (SEQS,), 0, ADAPTERS), jax.random.fold_in(splits[2], 1), 0, ADAPTERS - 1).astype(jnp.int32)
    cotangent = noise(splits[3], (SEQS, SEQ_LEN, D), 1.0, 6.0, ((0, 32),))
    norm_gain = jnp.clip(1.0 + 0.1 * jax.random.normal(splits[4], (3, D), jnp.float32), 0.5, 1.5)
    norm_bias = noise(splits[5], (3, D), 0.5, 3.0, (), jnp.float32)
    attention_weights = noise(splits[6], (6, D, D), D ** -0.5, 0.1875, ((1, 8),))
    output_weights = noise(splits[7], (2, D, D), (D // 16) ** -0.5, 0.75, ((1, 8),))
    expand_weight = noise(splits[8], (D, FF), D ** -0.5, 0.1875, ((0, 8),))
    contract_weight = noise(splits[9], (FF, D), FF ** -0.5, 0.09375, ((0, 8),))
    adapter_down = noise(splits[10], (8, ADAPTERS, D, RANK), D ** -0.5, 0.1875, ((2, 8),))
    adapter_up = noise(splits[11], (8, ADAPTERS, RANK, D), (RANK * 4) ** -0.5, 0.75, ((3, 8),))
    expand_down = noise(splits[12], (ADAPTERS, D, RANK), D ** -0.5, 0.1875, ((1, 8),))
    expand_up = noise(splits[13], (ADAPTERS, RANK, FF), (RANK * 4) ** -0.5, 0.75, ((2, 8),))
    contract_down = noise(splits[14], (ADAPTERS, FF, RANK), FF ** -0.5, 0.09375, ((1, 8),))
    contract_up = noise(splits[15], (ADAPTERS, RANK, D), (RANK * 4) ** -0.5, 0.75, ((2, 8),))
    return {"tokens": tokens, "encoder_states": encoder_states, "adapter_pick": adapter_pick, "cotangent": cotangent, "norm_gain": norm_gain, "norm_bias": norm_bias, "attention_weights": attention_weights, "output_weights": output_weights, "expand_weight": expand_weight, "contract_weight": contract_weight, "adapter_down": adapter_down, "adapter_up": adapter_up, "expand_down": expand_down, "expand_up": expand_up, "contract_down": contract_down, "contract_up": contract_up}


@jax.custom_vjp
def low(v):
    return lax.optimization_barrier(v.astype(jnp.bfloat16)).astype(jnp.float32)

@jax.custom_vjp
def low_back(v):
    return v

def low_keep(v):
    return (low(v), None)

def low_pass(kept, grad):
    return (grad,)

def back_keep(v):
    return (v, None)

def back_low(kept, grad):
    return (low(grad),)
low.defvjp(low_keep, low_pass)
low_back.defvjp(back_keep, back_low)
HIGHEST = lax.Precision.HIGHEST

def product(left, right):
    return jnp.dot(left, right, precision=HIGHEST)

def round_both(values):
    return low(low_back(values))

def layer_norm(values, gain, bias):
    centered = values - lax.optimization_barrier(jnp.mean(values, axis=-1, keepdims=True))
    variance = lax.optimization_barrier(jnp.mean(centered * centered, axis=-1, keepdims=True))
    return centered * lax.rsqrt(variance + 1e-05) * gain + bias

def gelu_value(values):
    return 0.5 * values * (1.0 + jax.scipy.special.erf(values * 0.7071067811865476))

def adapted(inputs, weight, down_stack, up_stack, onehot):
    down_pick = jnp.einsum('e,eir->ir', onehot, down_stack, precision=HIGHEST)
    up_pick = jnp.einsum('e,ero->ro', onehot, up_stack, precision=HIGHEST)
    return product(inputs, weight) + product(product(inputs, down_pick), up_pick)

def attention(queries, key_rows, value_rows, causal):
    query_count = queries.shape[0]
    key_count = key_rows.shape[0]
    query_heads = queries.reshape(query_count, HEADS, HDIM)
    key_heads = key_rows.reshape(key_count, HEADS, HDIM)
    value_heads = value_rows.reshape(key_count, HEADS, HDIM)
    scores = low_back(jnp.einsum('qhd,khd->hqk', query_heads, key_heads, precision=HIGHEST))
    if causal:
        allowed = jnp.arange(query_count, dtype=jnp.int32)[:, None] >= jnp.arange(key_count, dtype=jnp.int32)[None, :]
        scores = jnp.where(allowed[None], scores, -1e+30)
    chances = low(jax.nn.softmax(scores, axis=-1))
    result = jnp.einsum('hqk,khd->qhd', chances, value_heads, precision=HIGHEST)
    return result.reshape(query_count, HEADS * HDIM)

def decoder_layer(tokens_in, frames_in, adapters, onehot, frozen):
    norm_gain, norm_bias, attention_weights, output_weights, expand_weight, contract_weight = frozen
    adapter_down, adapter_up, expand_down, expand_up, contract_down, contract_up = adapters
    scaling = HDIM ** (-0.5)

    def through(inputs, position, weight):
        return adapted(inputs, weight, adapter_down[position], adapter_up[position], onehot)
    first = low(layer_norm(tokens_in, norm_gain[0], norm_bias[0]))
    queries = round_both(through(first, 0, attention_weights[0]) * scaling)
    key_rows = round_both(through(first, 1, attention_weights[1]))
    value_rows = round_both(through(first, 2, attention_weights[2]))
    mixed = round_both(attention(queries, key_rows, value_rows, True))
    middle = tokens_in + low_back(through(mixed, 6, output_weights[0]))
    second = low(layer_norm(middle, norm_gain[1], norm_bias[1]))
    cross_queries = round_both(through(second, 3, attention_weights[3]) * scaling)
    cross_keys = round_both(through(frames_in, 4, attention_weights[4]))
    cross_values = round_both(through(frames_in, 5, attention_weights[5]))
    cross_mixed = round_both(attention(cross_queries, cross_keys, cross_values, False))
    late = middle + low_back(through(cross_mixed, 7, output_weights[1]))
    third = low(layer_norm(late, norm_gain[2], norm_bias[2]))
    hidden = low_back(adapted(third, expand_weight, expand_down, expand_up, onehot))
    active = low(gelu_value(hidden))
    return late + low_back(adapted(active, contract_weight, contract_down, contract_up, onehot))

def reference(tokens, encoder_states, adapter_pick, cotangent, norm_gain, norm_bias, attention_weights, output_weights, expand_weight, contract_weight, adapter_down, adapter_up, expand_down, expand_up, contract_down, contract_up):
    frozen = tuple((argument.astype(jnp.float32) for argument in (norm_gain, norm_bias, attention_weights, output_weights, expand_weight, contract_weight)))
    adapters = tuple((argument.astype(jnp.float32) for argument in (adapter_down, adapter_up, expand_down, expand_up, contract_down, contract_up)))

    def one_sequence(totals, member):
        tokens_one, frames_one, picked, cotangent_one = member
        onehot = (jnp.arange(ADAPTERS, dtype=jnp.int32) == picked).astype(jnp.float32)

        def forward(tokens_in, frames_in, adapters_in):
            return decoder_layer(tokens_in, frames_in, adapters_in, onehot, frozen)
        result, pullback = jax.vjp(forward, tokens_one.astype(jnp.float32), frames_one.astype(jnp.float32), adapters)
        tokens_back, frames_back, adapter_back = pullback(cotangent_one.astype(jnp.float32))
        totals = jax.tree.map(jnp.add, totals, adapter_back)
        return (totals, (result.astype(jnp.bfloat16), tokens_back, frames_back))
    zeros = jax.tree.map(jnp.zeros_like, adapters)
    totals, stacked = lax.scan(one_sequence, zeros, (tokens, encoder_states, adapter_pick, cotangent))
    return (stacked[0], stacked[1], stacked[2], totals[0], totals[1], totals[2], totals[3], totals[4], totals[5])
```

```python
import functools

import jax
import jax.numpy as jnp
from jax import lax
from jax.experimental import pallas as pl
from jax.experimental.pallas import tpu as pltpu
from jax.sharding import PartitionSpec as P

HEADS = 16
HDIM = 64
ROOT_HALF = 0.7071067811865476
ROOT_TWOPI = 2.5066282746310002
BF16 = jnp.bfloat16
F32 = jnp.float32
AXES = ("rep", "shard")
BLOCKS = 4


def dot(left, right, over_left=1, over_right=0):
    return lax.dot_general(
        left, right, (((over_left,), (over_right,)), ((), ())), preferred_element_type=F32
    )


def pairs(move):
    found = []
    for rep in range(4):
        for shard in range(8):
            x, core, z, y = move(rep // 2, rep % 2, shard // 2, shard % 2)
            found.append((rep * 8 + shard, (2 * x + core) * 8 + 2 * (z % 4) + y))
    return found


Z_UP = pairs(lambda x, c, z, y: (x, c, z + 1, y))
Z_DOWN = pairs(lambda x, c, z, y: (x, c, z - 1, y))
Z_TWO = pairs(lambda x, c, z, y: (x, c, z + 2, y))
Y_SWAP = pairs(lambda x, c, z, y: (x, c, z, 1 - y))
X_SWAP = pairs(lambda x, c, z, y: (1 - x, c, z, y))
CORE_SWAP = pairs(lambda x, c, z, y: (x, 1 - c, z, y))


def move(value, pairing):
    return lax.ppermute(value, AXES, pairing)


def place():
    rep, shard = lax.axis_index("rep"), lax.axis_index("shard")
    return rep // 2, rep % 2, shard // 2, shard % 2


SOURCES = (0, 3, 1, 2)


def spread(own, forward_up):
    x, core, _, _ = place()
    count, rows, width = own.shape
    half, quarter = rows // 2, rows // 4
    mine = lax.dynamic_slice_in_dim(own, core * half, half, 1)
    below = move(mine, Z_UP)
    above = move(mine, Z_DOWN)
    across = move(below, Z_UP) if forward_up else move(above, Z_DOWN)
    column = jnp.stack(
        [lax.dynamic_slice_in_dim(v, x * quarter, quarter, 1) for v in (mine, below, above, across)]
    )
    beside = move(column, Y_SWAP)
    far = move(beside, X_SWAP)
    theirs = [move(v, CORE_SWAP) for v in (below, above, across, beside, far)]
    pieces = [own, below, above, across, beside, far] + theirs

    def body(own_ref, *refs):
        whole, sem = refs[-2:]
        below_r, above_r, across_r, beside_r, far_r = refs[:5]
        theirs_r = refs[5:10]
        x, core, z, y = place()
        copies = []

        def put(src, shard, offset, size):
            start = pl.multiple_of(shard * rows + offset, 16)
            copies.append(pltpu.make_async_copy(src, whole.at[:, pl.ds(start, size), :], sem))

        put(own_ref, 2 * z + y, 0, rows)
        for side, group in ((core, (below_r, above_r, across_r, beside_r, far_r)), (1 - core, theirs_r)):
            for k in range(1, 4):
                put(group[k - 1], 2 * ((z + SOURCES[k]) % 4) + y, side * half, half)
            for k in range(4):
                shard = 2 * ((z + SOURCES[k]) % 4) + 1 - y
                put(group[3].at[k], shard, side * half + x * quarter, quarter)
                put(group[4].at[k], shard, side * half + (1 - x) * quarter, quarter)
        for copy in copies:
            copy.start()
        for copy in copies:
            copy.wait()

    return pl.pallas_call(
        body,
        out_shape=jax.ShapeDtypeStruct((count, rows * 8, width), own.dtype),
        in_specs=[pl.BlockSpec(memory_space=pl.ANY)] * len(pieces),
        out_specs=pl.BlockSpec(memory_space=pltpu.VMEM),
        scratch_shapes=[pltpu.SemaphoreType.DMA],
    )(*pieces)


def in_order(pieces):
    _, _, z, y = place()
    stacked = jnp.stack(pieces)
    shards = jnp.arange(8, dtype=jnp.int32)
    distance = (shards // 2 - z) % 4
    slot = jnp.array([0, 2, 3, 1], jnp.int32)[distance]
    index = slot + jnp.where(shards % 2 == y, 0, 4)
    return jnp.take(stacked, index, axis=0)


def share_picks(pick):
    below = move(pick, Z_UP)
    above = move(pick, Z_DOWN)
    across = move(below, Z_UP)
    column = jnp.concatenate([pick, below, above, across])
    return column, move(column, Y_SWAP)


def fetch_adapters(table, column, beside):
    take = lambda e: lax.dynamic_index_in_dim(table, e, 0, keepdims=False)
    two = lambda k: jnp.stack([take(column[k]), take(beside[k])])
    to_below, to_above, to_across = two(1), two(2), two(3)
    above = move(to_below, Z_DOWN)
    below = move(to_above, Z_UP)
    across = move(to_across, Z_TWO)
    other = move(jnp.stack([take(beside[0]), below[1], above[1], across[1]]), Y_SWAP)
    pieces = [take(column[0]), below[0], above[0], across[0]] + [other[k] for k in range(4)]
    return in_order(pieces).transpose(1, 0, 2).reshape(table.shape[1], -1)


def return_grads(grads, column, beside, adapters):
    x, core, z, y = place()
    rows = grads.shape[0]
    sliced = grads.astype(BF16).reshape(rows, 4, 2, 128)
    shard_of = lambda k: (z + SOURCES[k]) % 4

    def part(k, lane):
        at_z = lax.dynamic_index_in_dim(sliced, shard_of(k), 1, keepdims=False)
        return lax.dynamic_index_in_dim(at_z, lane, 1, keepdims=False)

    mine = [part(k, y) for k in range(4)]
    theirs = move(jnp.stack([part(k, 1 - y) for k in range(4)]), Y_SWAP)
    pair = lambda k: jnp.stack([mine[k], theirs[k]])
    above = move(pair(1), Z_DOWN)
    below = move(pair(2), Z_UP)
    across = move(pair(3), Z_TWO)
    parts = [mine[0], below[0], above[0], across[0], theirs[0], below[1], above[1], across[1]]
    picks = [column[k] for k in range(4)] + [beside[k] for k in range(4)]
    ids = jnp.arange(adapters, dtype=jnp.int32)
    total = sum(
        (ids == p).astype(F32)[:, None, None] * v.astype(F32)[None] for p, v in zip(picks, parts)
    )
    half = adapters // 2
    low = total.astype(BF16)
    kept = lax.dynamic_slice_in_dim(total, core * half, half, 0)
    kept = kept + move(lax.dynamic_slice_in_dim(low, (1 - core) * half, half, 0), CORE_SWAP).astype(F32)
    kept = kept + move(kept.astype(BF16), X_SWAP).astype(F32)
    swapped = move(kept.astype(BF16), CORE_SWAP).astype(F32)
    both = jnp.concatenate([kept, swapped])
    return jnp.where(core == 0, both, jnp.concatenate([swapped, kept]))


def gelu_value(values):
    return 0.5 * values * (1.0 + lax.erf(values * ROOT_HALF))


def gelu_slope(values):
    return (
        0.5 * (1.0 + lax.erf(values * ROOT_HALF))
        + values * jnp.exp(-0.5 * values * values) / ROOT_TWOPI
    )


def norm_forward(values, gain, bias):
    centered = values - jnp.mean(values, axis=-1, keepdims=True)
    inverse = lax.rsqrt(jnp.mean(centered * centered, axis=-1, keepdims=True) + 1e-05)
    normed = centered * inverse
    return (normed * gain + bias, (normed, inverse))


def norm_backward(gradient, saved, gain):
    normed, inverse = saved
    scaled = gradient * gain
    centered = scaled - jnp.mean(scaled, axis=-1, keepdims=True)
    return inverse * (centered - normed * jnp.mean(scaled * normed, axis=-1, keepdims=True))


def project_forward(inputs, weight, down, up):
    reduced = dot(inputs, down, 1, 1).astype(BF16)
    return dot(inputs, weight) + dot(reduced, up), reduced


def project_backward(gradient, inputs, weight, down, up, reduced):
    narrow = dot(gradient, up, 1, 1).astype(BF16)
    result = dot(gradient, weight, 1, 1) + dot(narrow, down)
    return result, dot(narrow, inputs, 0, 0), dot(reduced, gradient, 0, 0)


def split_heads(values):
    rows = values.shape[0]
    return values.reshape(rows, HEADS // 4, 4, HDIM).transpose(1, 0, 2, 3)


def join_heads(values):
    return values.transpose(1, 0, 2, 3).reshape(values.shape[1], HEADS * HDIM)


def score_block(queries, key_rows, causal):
    scores = jnp.einsum("qhd,khd->hqk", queries, key_rows, preferred_element_type=F32)
    if causal:
        masked_out = lax.broadcasted_iota(jnp.int32, scores.shape, 2) > lax.broadcasted_iota(
            jnp.int32, scores.shape, 1
        )
        scores = jnp.where(masked_out, -1e30, scores)
    return scores


def attend_forward(queries, key_rows, value_rows, causal):
    def per_group(parts):
        group_query, group_keys, group_values = parts
        scores = score_block(group_query, group_keys, causal)
        highest = jnp.max(scores, axis=-1, keepdims=True)
        weights = jnp.exp(scores - highest)
        summed = jnp.sum(weights, axis=-1, keepdims=True)
        chances = (weights / summed).astype(BF16)
        result = jnp.einsum("hqk,khd->qhd", chances, group_values, preferred_element_type=F32)
        return (result.astype(BF16), (highest + jnp.log(summed))[..., 0])

    result, log_sums = lax.map(
        per_group, (split_heads(queries), split_heads(key_rows), split_heads(value_rows))
    )
    return (join_heads(result), log_sums)


def attend_backward(gradient, queries, key_rows, value_rows, log_sums, causal):
    def per_group(parts):
        group_grad, group_query, group_keys, group_values, group_log = parts
        scores = score_block(group_query, group_keys, causal)
        chances = jnp.exp(scores - group_log[..., None])
        chance_grad = jnp.einsum("qhd,khd->hqk", group_grad, group_values, preferred_element_type=F32)
        centered = chance_grad - jnp.sum(chances * chance_grad, axis=-1, keepdims=True)
        score_grad = (chances * centered).astype(BF16)
        query_grad = jnp.einsum("hqk,khd->qhd", score_grad, group_keys, preferred_element_type=F32)
        keys_grad = jnp.einsum("hqk,qhd->khd", score_grad, group_query, preferred_element_type=F32)
        values_grad = jnp.einsum(
            "hqk,qhd->khd", chances.astype(BF16), group_grad, preferred_element_type=F32
        )
        return (query_grad.astype(BF16), keys_grad.astype(BF16), values_grad.astype(BF16))

    grads = lax.map(
        per_group,
        (
            split_heads(gradient),
            split_heads(queries),
            split_heads(key_rows),
            split_heads(value_rows),
            log_sums,
        ),
    )
    return (join_heads(grads[0]), join_heads(grads[1]), join_heads(grads[2]))


EXPAND_DOWN, EXPAND_UP, CONTRACT_DOWN, CONTRACT_UP, TILES = 16, 17, 17 + BLOCKS, 17 + 2 * BLOCKS, 18 + 2 * BLOCKS
CHUNKS = ((4, 5), (0, 1, 2), (6, 3, 7), (8, 12, 9, 13), (10, 14, 11, 15))


def adapter_table(adapter_down, adapter_up, expand_down, expand_up, contract_down, contract_up):
    count, rank = adapter_down.shape[1], adapter_down.shape[3]
    lanes = adapter_down.shape[2]

    def blocked(values):
        cut = values.reshape(count, rank, BLOCKS, values.shape[2] // BLOCKS)
        return cut.transpose(0, 2, 1, 3).reshape(count, BLOCKS * rank, -1)

    return jnp.concatenate(
        [
            adapter_down.transpose(1, 0, 3, 2).reshape(count, -1, lanes),
            adapter_up.transpose(1, 0, 2, 3).reshape(count, -1, lanes),
            expand_down.transpose(0, 2, 1),
            blocked(expand_up),
            blocked(contract_down.transpose(0, 2, 1)),
            contract_up,
        ],
        axis=1,
    )


def table_outputs(total, lanes):
    count = total.shape[0]
    tiles = total.reshape(count, TILES, 16, lanes)

    def joined(values):
        return values.transpose(0, 2, 1, 3).reshape(count, 16, BLOCKS * lanes)

    return (
        tiles[:, 0:8].transpose(1, 0, 3, 2),
        tiles[:, 8:16].transpose(1, 0, 2, 3),
        tiles[:, EXPAND_DOWN].transpose(0, 2, 1),
        joined(tiles[:, EXPAND_UP : EXPAND_UP + BLOCKS]),
        joined(tiles[:, CONTRACT_DOWN : CONTRACT_DOWN + BLOCKS]).transpose(0, 2, 1),
        tiles[:, CONTRACT_UP],
    )


def layer(tokens, frames, cotangent, norm_gain, norm_bias, units, adapters, send):
    scaling = HDIM ** (-0.5)
    down = lambda p: adapters[p]
    up = lambda p: adapters[8 + p]
    reduced = {}
    grads = {}

    def forward(inputs, p):
        result, reduced[p] = project_forward(inputs, units[p], down(p), up(p))
        return result

    def backward(gradient, inputs, p):
        result, grads[p], grads[8 + p] = project_backward(
            gradient, inputs, units[p], down(p), up(p), reduced[p]
        )
        return result

    cross_keys = forward(frames, 4).astype(BF16)
    cross_values = forward(frames, 5).astype(BF16)
    residual = tokens.astype(F32)
    normed, norm_one = norm_forward(residual, norm_gain[0], norm_bias[0])
    first = normed.astype(BF16)
    queries = (forward(first, 0) * scaling).astype(BF16)
    key_rows = forward(first, 1).astype(BF16)
    value_rows = forward(first, 2).astype(BF16)
    mixed, log_one = attend_forward(queries, key_rows, value_rows, True)
    residual = residual + forward(mixed, 6)
    normed, norm_two = norm_forward(residual, norm_gain[1], norm_bias[1])
    second = normed.astype(BF16)
    cross_queries = (forward(second, 3) * scaling).astype(BF16)
    cross_mixed, log_two = attend_forward(cross_queries, cross_keys, cross_values, False)
    residual = residual + forward(cross_mixed, 7)
    normed, norm_three = norm_forward(residual, norm_gain[2], norm_bias[2])
    third = normed.astype(BF16)

    opened = dot(third, adapters[EXPAND_DOWN], 1, 1).astype(BF16)
    closing = dot(cotangent, adapters[CONTRACT_UP], 1, 1).astype(BF16)
    branch = jnp.zeros(residual.shape, F32)
    closed = jnp.zeros((third.shape[0], 16), F32)
    third_grad = jnp.zeros(residual.shape, F32)
    opening = jnp.zeros((third.shape[0], 16), F32)
    for b in range(BLOCKS):
        expand, contract = units[8 + b], units[12 + b]
        expand_up, contract_down = adapters[EXPAND_UP + b], adapters[CONTRACT_DOWN + b]
        hidden = dot(third, expand) + dot(opened, expand_up)
        active = gelu_value(hidden).astype(BF16)
        branch = branch + dot(active, contract)
        closed = closed + dot(active, contract_down, 1, 1)
        active_grad = dot(cotangent, contract, 1, 1) + dot(closing, contract_down)
        hidden_grad = (active_grad * gelu_slope(hidden)).astype(BF16)
        third_grad = third_grad + dot(hidden_grad, expand, 1, 1)
        opening = opening + dot(hidden_grad, expand_up, 1, 1)
        grads[EXPAND_UP + b] = dot(opened, hidden_grad, 0, 0)
        grads[CONTRACT_DOWN + b] = dot(closing, active, 0, 0)
    closed, opening = closed.astype(BF16), opening.astype(BF16)
    branch = branch + dot(closed, adapters[CONTRACT_UP])
    third_grad = third_grad + dot(opening, adapters[EXPAND_DOWN])
    grads[CONTRACT_UP] = dot(closed, cotangent, 0, 0)
    grads[EXPAND_DOWN] = dot(opening, third, 0, 0)
    result = (residual + branch).astype(BF16)

    late_grad = cotangent.astype(F32) + norm_backward(third_grad, norm_three, norm_gain[2])
    cross_mixed_grad = backward(late_grad.astype(BF16), cross_mixed, 7).astype(BF16)
    query_grad, keys_grad, values_grad = attend_backward(
        cross_mixed_grad, cross_queries, cross_keys, cross_values, log_two, False
    )
    second_grad = backward(query_grad * scaling, second, 3)
    frame_grad = backward(keys_grad, frames, 4) + backward(values_grad, frames, 5)
    middle_grad = late_grad + norm_backward(second_grad, norm_two, norm_gain[1])
    mixed_grad = backward(middle_grad.astype(BF16), mixed, 6).astype(BF16)
    query_grad, keys_grad, values_grad = attend_backward(
        mixed_grad, queries, key_rows, value_rows, log_one, True
    )
    first_grad = backward(query_grad * scaling, first, 0)
    first_grad = first_grad + backward(keys_grad, first, 1)
    first_grad = first_grad + backward(values_grad, first, 2)
    token_grad = middle_grad + norm_backward(first_grad, norm_one, norm_gain[0])
    total = send(grads)
    return result, token_grad, frame_grad, total


def on_device(
    ring,
    tokens,
    encoder_states,
    adapter_pick,
    cotangent,
    norm_gain,
    norm_bias,
    attention_weights,
    output_weights,
    expand_weight,
    contract_weight,
    adapter_down,
    adapter_up,
    expand_down,
    expand_up,
    contract_down,
    contract_up,
):
    adapters = adapter_down.shape[1]
    lanes = adapter_down.shape[2]
    shards = tokens.shape[2] // lanes
    table = adapter_table(adapter_down, adapter_up, expand_down, expand_up, contract_down, contract_up)
    if ring:
        column, beside = share_picks(adapter_pick)
        picked = fetch_adapters(table, column, beside)
        wide, deep = expand_weight.shape[1] // shards, contract_weight.shape[0]
        step = deep // BLOCKS

        def own(unit):
            if unit < 6:
                return attention_weights[unit]
            if unit < 8:
                return output_weights[unit - 6]
            if unit < 12:
                first = (unit - 8) * step
                return jnp.concatenate(
                    [expand_weight[:, s * wide + first : s * wide + first + step] for s in range(shards)],
                    axis=1,
                )
            return contract_weight[(unit - 12) * step : (unit - 11) * step]

        units = {}
        for number, chunk in enumerate(CHUNKS):
            whole = spread(jnp.stack([own(unit) for unit in chunk]), number % 2 == 0)
            for at, unit in enumerate(chunk):
                units[unit] = whole[at]

        def send(grads):
            flat = jnp.concatenate([grads[k] for k in range(TILES)])
            return return_grads(flat, column, beside, adapters)

    else:
        gather = lambda v, axis: lax.all_gather(v, "shard", axis=axis, tiled=True)
        attention, output = gather(attention_weights, 1), gather(output_weights, 1)
        expand, contract = gather(expand_weight, 0), gather(contract_weight, 0)
        units = {p: attention[p] for p in range(6)} | {6 + p: output[p] for p in range(2)}
        step = contract_weight.shape[0] // BLOCKS
        cut = expand.reshape(expand.shape[0], shards, BLOCKS, step)
        deep = contract.reshape(shards, BLOCKS, step, -1)
        for b in range(BLOCKS):
            units[8 + b] = cut[:, :, b].reshape(expand.shape[0], -1)
            units[12 + b] = deep[:, b].reshape(-1, contract.shape[1])
        mine = lax.all_gather(table, "shard", axis=2, tiled=True)
        picked = lax.dynamic_index_in_dim(mine, adapter_pick[0], 0, keepdims=False)

        def send(grads):
            flat = jnp.concatenate([grads[k] for k in range(TILES)])
            hot = (jnp.arange(adapters, dtype=jnp.int32) == adapter_pick[0]).astype(F32)
            owned = lax.psum_scatter(
                hot[:, None, None] * flat[None], "shard", scatter_dimension=2, tiled=True
            )
            return lax.psum(owned.astype(BF16), "rep").astype(F32)

    result, token_grad, frame_grad, total = layer(
        tokens[0],
        encoder_states[0],
        cotangent[0],
        norm_gain,
        norm_bias,
        units,
        picked.reshape(TILES, 16, -1),
        send,
    )
    return (result[None], token_grad[None], frame_grad[None]) + table_outputs(total, lanes)


def solution(mesh):
    ring = mesh.shape["rep"] == 4 and mesh.shape["shard"] == 8
    both = P(AXES, None, None)
    maps = (
        P(None, None, "shard", None),
        P(None, None, None, "shard"),
        P(None, "shard", None),
        P(None, None, "shard"),
        P(None, "shard", None),
        P(None, None, "shard"),
    )
    placed = (
        both,
        both,
        P(AXES),
        both,
        P(),
        P(),
        P(None, "shard", None),
        P(None, "shard", None),
        P("shard", None),
        P("shard", None),
    ) + maps
    return jax.shard_map(
        functools.partial(on_device, ring),
        mesh=mesh,
        in_specs=placed,
        out_specs=(both, both, both) + maps,
        check_vma=False,
    )
```
